128 devices in a mesh: seq: 32 (over z, x, core), dp: 4 (over y).
Axes of the slice: x: 4, y: 4, z: 4, core: 2. Of those that a mesh axis runs over, the one named last changes fastest.
Arguments:
- queries: bfloat16 [4, 8192, 1024], P('dp', 'seq'), may hold values from -8 to 8
- key_rows: bfloat16 [4, 8192, 1024], P('dp', 'seq'), may hold values from -8 to 8
- value_rows: bfloat16 [4, 8192, 1024], P('dp', 'seq'), may hold values from -16 to 16
- conv_key: float32 [5, 4, 1024], replicated, may hold values from -2.5 to 2.5
- conv_value: float32 [5, 4, 1024], replicated, may hold values from -2.5 to 2.5
- grad_out: bfloat16 [4, 8192, 1024], P('dp', 'seq'), may hold values from -12 to 12
Outputs:
- attended: bfloat16 [4, 8192, 1024], P('dp', 'seq')
- grad_query: bfloat16 [4, 8192, 1024], P('dp', 'seq')
- grad_key: bfloat16 [4, 8192, 1024], P('dp', 'seq')
- grad_value: bfloat16 [4, 8192, 1024], P('dp', 'seq')
- grad_conv_key: float32 [5, 4, 1024], replicated
- grad_conv_value: float32 [5, 4, 1024], replicated
The draws below stay inside these ranges and needn't reach their ends.
All inputs are finite; a program needn't handle non-finite values.
Results may differ from the reference program's by a relative error of at most 0.019.
Values may be sent and summed in bfloat16 or wider, within the bound.
No kernel may reach another device: no remote copies, remote signals or barrier semaphores. Data moves between devices by JAX's collectives and lax.ppermute only.
A program may use at most 128 MiB of HBM per device.

```python
import jax
import jax.numpy as jnp
from jax import lax

HEADS = 8
HEAD_DIM = 128
BLOCK = 128
D = 1024
LEVELS = 5
SEQLEN = 8192
BATCH = 4


def draw_queries(key, part):
    base_key = jax.random.fold_in(key, 11)
    drawn = jnp.clip(1.5 * jax.random.normal(base_key, (BATCH, SEQLEN, D), jnp.float32), -7.5, 7.5)
    return drawn.astype(jnp.bfloat16)


def draw_key_rows(key, part):
    base_key = jax.random.fold_in(key, 13)
    drawn = jnp.clip(jax.random.normal(base_key, (BATCH, SEQLEN, D), jnp.float32), -6.0, 6.0)
    return drawn.astype(jnp.bfloat16)


def levels(rng, extent, shards, least, high):
    def one(dim, parts):
        heights = jax.random.uniform(jax.random.fold_in(jax.random.fold_in(rng, 6), dim), (parts,), jnp.float32, least / len(shards), high / len(shards))
        return jnp.repeat(jnp.exp(heights), extent[dim] // parts).reshape((-1,) + (1,) * (len(extent) - dim - 1))

    loudness = one(*shards[0])
    for cut in shards[1:]:
        loudness = loudness * one(*cut)
    return loudness


def gaussian(rng, dims, scale, limit, split=(), held_as=jnp.bfloat16):
    values = jax.random.normal(rng, dims, jnp.float32) * scale
    if len(split) > 0:
        values = levels(rng, dims, split, -0.22, 0.18) * values
    return jnp.clip(values, min=-limit, max=limit).astype(held_as)


def setup_inputs(seed: int = 0) -> dict:
    streams_of = jax.random.split(jax.random.key(seed), 7)
    queries = draw_queries(jax.random.fold_in(streams_of[6], 71), 0)
    key_rows = draw_key_rows(jax.random.fold_in(streams_of[6], 71), 0)
    value_rows = gaussian(streams_of[2], (BATCH, SEQLEN, D), 4.0, 16.0, ((0, 4), (1, 32)))
    conv_key = gaussian(streams_of[3], (LEVELS, 4, D), 0.5, 2.5, (), jnp.float32)
    conv_value = gaussian(streams_of[4], (LEVELS, 4, D), 0.5, 2.5, (), jnp.float32)
    grad_out = gaussian(streams_of[5], (BATCH, SEQLEN, D), 2.0, 12.0, ((0, 4), (1, 32)))
    return dict(queries=queries, key_rows=key_rows, value_rows=value_rows, conv_key=conv_key, conv_value=conv_value, grad_out=grad_out)


def coarsen(extended, weight):
    out_rows = (extended.shape[0] - 2) // 2
    summed = weight[0] * extended[0:2 * out_rows:2].astype(jnp.float32)
    for offset in range(1, 4):
        summed = summed + weight[offset] * extended[offset:offset + 2 * out_rows:2].astype(jnp.float32)
    return summed.astype(jnp.bfloat16)


def coarsen_back(upstream, extended, weight):
    out_rows, feat_width = upstream.shape
    zero_row = jnp.zeros((1, feat_width), jnp.float32)
    even_rows = jnp.concatenate([weight[0] * upstream, zero_row], 0) + jnp.concatenate([zero_row, weight[2] * upstream], 0)
    odd_rows = jnp.concatenate([weight[1] * upstream, zero_row], 0) + jnp.concatenate([zero_row, weight[3] * upstream], 0)
    spread = jnp.stack([even_rows, odd_rows], 1).reshape(2 * out_rows + 2, feat_width)
    weight_grad = jnp.stack([jnp.sum(upstream * extended[offset:offset + 2 * out_rows:2].astype(jnp.float32), 0) for offset in range(4)])
    return spread, weight_grad


def one_sequence(queries, key_rows, value_rows, grad_out, conv_key, conv_value):
    seq_rows, feat_width = queries.shape
    fine_blocks = seq_rows // BLOCK
    score_scale = HEAD_DIM ** -0.5
    zero_pair = jnp.zeros((2, feat_width), jnp.bfloat16)
    pad_rows = jnp.zeros((BLOCK, feat_width), jnp.bfloat16)
    key_levels = [key_rows]
    value_levels = [value_rows]
    for level_id in range(LEVELS):
        key_levels.append(coarsen(jnp.concatenate([zero_pair, key_levels[-1]], 0), conv_key[level_id]))
        value_levels.append(coarsen(jnp.concatenate([zero_pair, value_levels[-1]], 0), conv_value[level_id]))
    key_padded = [jnp.concatenate([pad_rows, level_rows, pad_rows], 0) for level_rows in key_levels]
    value_padded = [jnp.concatenate([pad_rows, level_rows, pad_rows], 0) for level_rows in value_levels]
    key_count = (3 + 2 * LEVELS) * BLOCK

    def step(scan_state, block_id):
        key_grads, value_grads = scan_state
        key_spans = [(0, (block_id * BLOCK).astype(jnp.int32), 3 * BLOCK)]
        key_masks = [jnp.full((BLOCK,), block_id >= 1), jnp.ones((BLOCK,), jnp.bool_), jnp.full((BLOCK,), block_id + 1 < fine_blocks)]
        for level_id in range(1, LEVELS + 1):
            coarse_id = block_id // (2 ** level_id)
            key_spans.append((level_id, (coarse_id * BLOCK).astype(jnp.int32), BLOCK))
            key_masks.append(jnp.full((BLOCK,), coarse_id >= 1))
            key_spans.append((level_id, ((coarse_id + 2) * BLOCK).astype(jnp.int32), BLOCK))
            key_masks.append(jnp.full((BLOCK,), coarse_id + 1 < fine_blocks // (2 ** level_id)))
        key_set = jnp.concatenate([lax.dynamic_slice_in_dim(key_padded[level_id], start_row, span_rows, 0) for level_id, start_row, span_rows in key_spans], 0)
        value_set = jnp.concatenate([lax.dynamic_slice_in_dim(value_padded[level_id], start_row, span_rows, 0) for level_id, start_row, span_rows in key_spans], 0)
        valid_mask = jnp.concatenate(key_masks, 0)
        key_set = key_set.astype(jnp.float32).reshape(key_count, HEADS, HEAD_DIM)
        value_set = value_set.astype(jnp.float32).reshape(key_count, HEADS, HEAD_DIM)
        start_fine = (block_id * BLOCK).astype(jnp.int32)
        query_block = lax.dynamic_slice_in_dim(queries, start_fine, BLOCK, 0).astype(jnp.float32).reshape(BLOCK, HEADS, HEAD_DIM)
        out_block = lax.dynamic_slice_in_dim(grad_out, start_fine, BLOCK, 0).astype(jnp.float32).reshape(BLOCK, HEADS, HEAD_DIM)
        raw_scores = jnp.einsum('qhe,khe->hqk', query_block, key_set, precision=lax.Precision.HIGHEST) * score_scale
        raw_scores = jnp.where(valid_mask[None, None, :], raw_scores, -jnp.inf)
        row_max = jnp.max(raw_scores, -1, keepdims=True)
        exp_scores = jnp.exp(raw_scores - row_max)
        prob_full = exp_scores / jnp.sum(exp_scores, -1, keepdims=True)
        probs_low = prob_full.astype(jnp.bfloat16).astype(jnp.float32)
        attended = jnp.einsum('hqk,khe->qhe', probs_low, value_set, precision=lax.Precision.HIGHEST).reshape(BLOCK, feat_width).astype(jnp.bfloat16)
        grad_prob = jnp.einsum('qhe,khe->hqk', out_block, value_set, precision=lax.Precision.HIGHEST)
        row_delta = jnp.sum(prob_full * grad_prob, -1, keepdims=True)
        dscore = (prob_full * (grad_prob - row_delta) * score_scale).astype(jnp.bfloat16).astype(jnp.float32)
        grad_q = jnp.einsum('hqk,khe->qhe', dscore, key_set, precision=lax.Precision.HIGHEST).reshape(BLOCK, feat_width).astype(jnp.bfloat16)
        key_part = jnp.einsum('hqk,qhe->khe', dscore, query_block, precision=lax.Precision.HIGHEST).reshape(key_count, feat_width)
        value_part = jnp.einsum('hqk,qhe->khe', probs_low, out_block, precision=lax.Precision.HIGHEST).reshape(key_count, feat_width)
        key_grads = list(key_grads)
        value_grads = list(value_grads)
        offset = 0
        for level_id, start_row, span_rows in key_spans:
            current = lax.dynamic_slice_in_dim(key_grads[level_id], start_row, span_rows, 0)
            key_grads[level_id] = lax.dynamic_update_slice_in_dim(key_grads[level_id], current + key_part[offset:offset + span_rows], start_row, 0)
            current = lax.dynamic_slice_in_dim(value_grads[level_id], start_row, span_rows, 0)
            value_grads[level_id] = lax.dynamic_update_slice_in_dim(value_grads[level_id], current + value_part[offset:offset + span_rows], start_row, 0)
            offset += span_rows
        return (tuple(key_grads), tuple(value_grads)), (attended, grad_q)

    start_state = (tuple(jnp.zeros(level_rows.shape, jnp.float32) for level_rows in key_padded), tuple(jnp.zeros(level_rows.shape, jnp.float32) for level_rows in value_padded))
    final_state, outputs = lax.scan(step, start_state, jnp.arange(fine_blocks, dtype=jnp.int32))
    key_grads, value_grads = final_state
    attended_all = outputs[0].reshape(seq_rows, feat_width)
    grad_q_all = outputs[1].reshape(seq_rows, feat_width)
    key_flow = key_grads[LEVELS][BLOCK:-BLOCK]
    value_flow = value_grads[LEVELS][BLOCK:-BLOCK]
    key_weight_grads = [None] * LEVELS
    value_weight_grads = [None] * LEVELS
    for level_id in range(LEVELS, 0, -1):
        spread, key_weight_grads[level_id - 1] = coarsen_back(key_flow, jnp.concatenate([zero_pair, key_levels[level_id - 1]], 0), conv_key[level_id - 1])
        key_flow = key_grads[level_id - 1][BLOCK:-BLOCK] + spread[2:]
        spread, value_weight_grads[level_id - 1] = coarsen_back(value_flow, jnp.concatenate([zero_pair, value_levels[level_id - 1]], 0), conv_value[level_id - 1])
        value_flow = value_grads[level_id - 1][BLOCK:-BLOCK] + spread[2:]
    return attended_all, grad_q_all, key_flow.astype(jnp.bfloat16), value_flow.astype(jnp.bfloat16), jnp.stack(key_weight_grads), jnp.stack(value_weight_grads)


def reference(queries, key_rows, value_rows, conv_key, conv_value, grad_out):
    def per_sequence(seq_items):
        return one_sequence(seq_items[0], seq_items[1], seq_items[2], seq_items[3], conv_key, conv_value)

    results = lax.map(per_sequence, (queries, key_rows, value_rows, grad_out))
    return results[0], results[1], results[2], results[3], jnp.sum(results[4], 0), jnp.sum(results[5], 0)
```

```python
import functools
import math

import jax
import jax.numpy as jnp
from jax import lax
from jax.experimental import pallas as pl
from jax.experimental.pallas import tpu as pltpu
from jax.sharding import Mesh, PartitionSpec as P

HD = 128
BLK = 128
LEVELS = 5
NZ, NX, NC, NY = 4, 4, 2, 4
ROWS = 256
GROUP = ROWS * NX * NC
PAIRS = GROUP // 256
SIZES = [GROUP >> l for l in range(LEVELS + 1)]
HALO = [64 >> l for l in range(LEVELS + 1)]
PRE = 8
OFFS = [0]
for _l in range(LEVELS):
    OFFS.append(OFFS[-1] + SIZES[_l] + 2 * BLK)
TOTAL = OFFS[LEVELS] + BLK
NBLK = TOTAL // BLK
KEYS = 4 * BLK + 8 * BLK + BLK
SCALE = HD ** -0.5
EXPC = SCALE * math.log2(math.e)
NEG = -1e30
F32 = jnp.float32
BF16 = jnp.bfloat16
PARAMS = pltpu.CompilerParams(vmem_limit_bytes=56 << 20)


def nn(a, b):
    return lax.dot_general(a, b, (((1,), (0,)), ((), ())), preferred_element_type=F32)


def nt(a, b):
    return lax.dot_general(a, b, (((1,), (1,)), ((), ())), preferred_element_type=F32)


def chunks(total, step):
    return [(r, min(step, total - r)) for r in range(0, total, step)]


def coarse_kernel(z_ref, *refs):
    srcs, halos, weights = refs[0:2], refs[2:4], refs[4:6]
    outs = refs[6:]
    has_left = (z_ref[0] > 0).astype(F32)
    per = LEVELS * 2
    for side in range(2):
        src, halo, weight = srcs[side], halos[side], weights[side]
        wide = outs[side * per : side * per + LEVELS]
        own = outs[side * per + LEVELS : (side + 1) * per]
        x = wide[0]
        x[0:PRE, :] = jnp.zeros((PRE, HD), F32)
        x[PRE : PRE + HALO[0], :] = halo[...].astype(F32) * has_left
        for r, n in chunks(GROUP, 256):
            x[PRE + HALO[0] + r : PRE + HALO[0] + r + n, :] = src[r : r + n, :].astype(F32)
        for level in range(1, LEVELS + 1):
            x = wide[level - 1]
            taps = [weight[4 * (level - 1) + j : 4 * (level - 1) + j + 1, :] for j in range(4)]
            if level < LEVELS:
                wide[level][0:PRE, :] = jnp.zeros((PRE, HD), F32)
            first = 0 if level < LEVELS else HALO[level]
            for r, n in chunks(HALO[level] + SIZES[level] - first, 128):
                r += first
                acc = None
                for j in range(4):
                    term = taps[j] * x[pl.ds(PRE + 2 * r - 2 + j, n, stride=2), :]
                    acc = term if acc is None else acc + term
                low = acc.astype(BF16)
                if level < LEVELS:
                    wide[level][PRE + r : PRE + r + n, :] = low.astype(F32)
                else:
                    own[level - 1][r - first : r - first + n, :] = low
            if level < LEVELS:
                for r, n in chunks(SIZES[level], 256):
                    start = PRE + HALO[level] + r
                    own[level - 1][r : r + n, :] = wide[level][start : start + n, :].astype(BF16)


def attention_kernel(z_ref, q_ref, do_ref, *refs):
    own_k = refs[0:LEVELS]
    own_v = refs[LEVELS : 2 * LEVELS]
    rim_l, rim_r, far = refs[2 * LEVELS : 2 * LEVELS + 3]
    att_ref, dq_ref, gl_ref, gr_ref, gfar_ref, dk_ref, dv_ref = refs[2 * LEVELS + 3 : 2 * LEVELS + 10]
    kx, vx, kt, vt, s_ref, e_ref = refs[2 * LEVELS + 10 :]
    z = z_ref[0]
    for side, (own, ext, tr, grad) in enumerate(((own_k, kx, kt, dk_ref), (own_v, vx, vt, dv_ref))):
        for level in range(LEVELS):
            off = OFFS[level]
            ext[off : off + BLK, :] = rim_l[level, side]
            for r, n in chunks(SIZES[level], 256):
                ext[off + BLK + r : off + BLK + r + n, :] = own[level][r : r + n, :]
            end = off + BLK + SIZES[level]
            ext[end : end + BLK, :] = rim_r[level, side]
        ext[OFFS[LEVELS] : TOTAL, :] = far[side]

        def prepare(i, _, ext=ext, tr=tr, grad=grad):
            rows = pl.ds(pl.multiple_of(i * BLK, BLK), BLK)
            tr[i] = ext[rows, :].T
            grad[rows, :] = jnp.zeros((BLK, HD), F32)
            return 0

        lax.fori_loop(0, NBLK, prepare, 0)

    lane = lax.broadcasted_iota(jnp.int32, (BLK, 2 * BLK), 1)

    def pair(p, _):
        qrows = pl.ds(pl.multiple_of(p * 256, 256), 256)
        qt = q_ref[qrows, :].T
        dot_t = do_ref[qrows, :].astype(F32).T
        groups = [[2 * p + i for i in range(4)]]
        valid = [None]
        for level in range(1, LEVELS):
            c = p >> (level - 1)
            base = OFFS[level] // BLK
            groups.append([base + c, base + c + 2])
            count = SIZES[level] // BLK
            valid.append((jnp.logical_or(c > 0, z > 0), jnp.logical_or(c < count - 1, z < NZ - 1)))
        groups.append([OFFS[LEVELS] // BLK])
        valid.append((None,))

        def rows_of(ext, blocks, contiguous):
            if contiguous:
                return ext[pl.ds(pl.multiple_of(blocks[0] * BLK, BLK), BLK * len(blocks)), :]
            parts = [ext[pl.ds(pl.multiple_of(b * BLK, BLK), BLK), :] for b in blocks]
            return parts[0] if len(parts) == 1 else jnp.concatenate(parts, 0)

        def cols_of(tr, blocks):
            parts = [tr[b] for b in blocks]
            return parts[0] if len(parts) == 1 else jnp.concatenate(parts, 1)

        top = jnp.full((8, 256), NEG, F32)
        row = 0
        for gid, blocks in enumerate(groups):
            n = BLK * len(blocks)
            s = nn(rows_of(kx, blocks, gid == 0), qt)
            for i in range(len(blocks)):
                part = s[i * BLK : (i + 1) * BLK, :]
                if gid == 0 and i == 0:
                    lim = jnp.where(jnp.logical_or(p > 0, z > 0), BLK, 0)
                    part = jnp.where(lane < lim, part, NEG)
                elif gid == 0 and i == 3:
                    lim = jnp.where(jnp.logical_or(p < PAIRS - 1, z < NZ - 1), BLK, 2 * BLK)
                    part = jnp.where(lane >= lim, part, NEG)
                elif gid > 0 and valid[gid][i] is not None:
                    part = jnp.where(valid[gid][i], part, NEG)
                s_ref[row + i * BLK : row + (i + 1) * BLK, :] = part
                top = jnp.maximum(top, jnp.max(part.reshape(BLK // 8, 8, 256), 0))
            row += n
        shift = jnp.max(top, 0, keepdims=True) * EXPC
        total = jnp.zeros((8, 256), F32)
        out_t = jnp.zeros((HD, 256), F32)
        row = 0
        for gid, blocks in enumerate(groups):
            n = BLK * len(blocks)
            e = jnp.exp2(s_ref[row : row + n, :] * EXPC - shift)
            total = total + jnp.sum(e.reshape(n // 8, 8, 256), 0)
            low = e.astype(BF16)
            e_ref[row : row + n, :] = low
            out_t = out_t + nn(cols_of(vt, blocks), low)
            row += n
        inverse = 1.0 / jnp.sum(total, 0, keepdims=True)
        out_t = out_t * inverse
        att_ref[qrows, :] = out_t.T.astype(BF16)
        don_t = (dot_t * inverse).astype(BF16)
        delta = jnp.sum(don_t.astype(F32) * out_t, 0, keepdims=True)
        dq_t = jnp.zeros((HD, 256), F32)
        row = 0
        for gid, blocks in enumerate(groups):
            n = BLK * len(blocks)
            low = e_ref[row : row + n, :]
            dp = nn(rows_of(vx, blocks, gid == 0), don_t)
            ds = (low.astype(F32) * (dp - delta)).astype(BF16)
            dq_t = dq_t + nn(cols_of(kt, blocks), ds)
            dk = nt(ds, qt)
            dv = nt(low, don_t)
            for i, b in enumerate(blocks):
                rows = pl.ds(pl.multiple_of(b * BLK, BLK), BLK)
                dk_ref[rows, :] += dk[i * BLK : (i + 1) * BLK, :]
                dv_ref[rows, :] += dv[i * BLK : (i + 1) * BLK, :]
            row += n
        dq_ref[qrows, :] = (dq_t * SCALE).T.astype(BF16)
        return 0

    lax.fori_loop(0, PAIRS, pair, 0)
    for level in range(LEVELS):
        off = OFFS[level]
        end = off + BLK + SIZES[level]
        gl_ref[level, 0] = (dk_ref[off : off + BLK, :] * SCALE).astype(BF16)
        gl_ref[level, 1] = dv_ref[off : off + BLK, :].astype(BF16)
        gr_ref[level, 0] = (dk_ref[end : end + BLK, :] * SCALE).astype(BF16)
        gr_ref[level, 1] = dv_ref[end : end + BLK, :].astype(BF16)
    gfar_ref[0] = (dk_ref[OFFS[LEVELS] : TOTAL, :] * SCALE).astype(BF16)
    gfar_ref[1] = dv_ref[OFFS[LEVELS] : TOTAL, :].astype(BF16)


def back_kernel(dk_ref, dv_ref, from_left, from_right, far_a, far_b, wk_ref, wv_ref, *refs):
    xs = (refs[0:LEVELS], refs[LEVELS : 2 * LEVELS])
    fine_outs, halo_out, gw_outs = refs[2 * LEVELS : 2 * LEVELS + 2], refs[2 * LEVELS + 2], refs[2 * LEVELS + 3 : 2 * LEVELS + 5]
    g = refs[2 * LEVELS + 5 :]
    for side in range(2):
        weight = (wk_ref, wv_ref)[side]
        grad = (dk_ref, dv_ref)[side]
        mult = (SCALE, 1.0)[side]
        fine_out, gw_out = fine_outs[side], gw_outs[side]
        end = HALO[LEVELS] + SIZES[LEVELS]
        g[LEVELS][0 : HALO[LEVELS], :] = jnp.zeros((HALO[LEVELS], HD), F32)
        g[LEVELS][HALO[LEVELS] : end, :] = far_a[side].astype(F32) + far_b[side].astype(F32)
        g[LEVELS][end : end + 8, :] = jnp.zeros((8, HD), F32)
        for level in range(LEVELS, 0, -1):
            taps = [weight[4 * (level - 1) + j : 4 * (level - 1) + j + 1, :] for j in range(4)]
            x = xs[side][level - 1]
            here, below = g[level], g[level - 1]
            sums = [jnp.zeros((8, HD), F32) for _ in range(4)]
            total = HALO[level] + SIZES[level]
            for r, n in chunks(total, 128):
                g0 = here[r : r + n, :]
                g1 = here[r + 1 : r + n + 1, :]
                below[pl.ds(2 * r, n, stride=2), :] = taps[2] * g0 + taps[0] * g1
                below[pl.ds(2 * r + 1, n, stride=2), :] = taps[3] * g0 + taps[1] * g1
                for j in range(4):
                    prod = g0 * x[pl.ds(PRE + 2 * r - 2 + j, n, stride=2), :]
                    if n % 8 == 0:
                        sums[j] = sums[j] + jnp.sum(prod.reshape(n // 8, 8, HD), 0)
                    else:
                        gap = jnp.zeros((8 - n % 8, HD), F32)
                        prod = jnp.concatenate([prod, gap], 0)
                        sums[j] = sums[j] + jnp.sum(prod.reshape((n + 7) // 8, 8, HD), 0)
            for j in range(4):
                gw_out[4 * (level - 1) + j : 4 * (level - 1) + j + 1, :] = jnp.sum(sums[j], 0, keepdims=True)
            low = level - 1
            off = OFFS[low] + BLK
            size, pad = SIZES[low], HALO[low]
            for r, n in chunks(size, 128):
                value = below[pad + r : pad + r + n, :] + grad[off + r : off + r + n, :] * mult
                if r == 0:
                    value = value + from_left[low, side].astype(F32)
                if r == size - BLK:
                    value = value + from_right[low, side].astype(F32)
                if low > 0:
                    below[pad + r : pad + r + n, :] = value
                else:
                    fine_out[r : r + n, :] = value.astype(BF16)
            if low > 0:
                below[pad + size : pad + size + 8, :] = jnp.zeros((8, HD), F32)
            else:
                halo_out[side] = below[0:pad, :].astype(BF16)


def ring(axis, k, size=4):
    return [(i, (i + k) % size) for i in range(size)]


def swap_core(value):
    return lax.ppermute(value, "c", [(0, 1), (1, 0)])


def take(value, index, dim):
    return lax.dynamic_index_in_dim(value, index, dim, keepdims=False)


def rows_to_heads(arrays):
    n = len(arrays)
    x, c = lax.axis_index("x"), lax.axis_index("c")
    stacked = jnp.stack([a.reshape(ROWS, NX, NC, HD) for a in arrays], 0)
    by_head = stacked.transpose(2, 3, 0, 1, 4)
    keep, give = take(by_head, c, 1), take(by_head, 1 - c, 1)
    got = swap_core(give)
    both = jnp.stack([jnp.where(c == 0, keep, got), jnp.where(c == 0, got, keep)], 2)
    whole = jnp.zeros((n, NX, NC, ROWS, HD), BF16)
    for k in (0, 1, 3, 2):
        piece = take(both, (x + k) % NX, 0)
        if k:
            piece = lax.ppermute(piece, "x", ring("x", k))
        whole = lax.dynamic_update_slice_in_dim(whole, piece[:, None], (x - k) % NX, 1)
    return [whole[i].reshape(GROUP, HD) for i in range(n)]


def heads_to_rows(arrays):
    n = len(arrays)
    x, c = lax.axis_index("x"), lax.axis_index("c")
    stacked = jnp.stack([a.reshape(NX, NC, ROWS, HD) for a in arrays], 1)
    whole = jnp.zeros((NX, n, NC, ROWS, HD), BF16)
    for k in (0, 1, 3, 2):
        piece = take(stacked, (x + k) % NX, 0)
        if k:
            piece = lax.ppermute(piece, "x", ring("x", k))
        whole = lax.dynamic_update_slice_in_dim(whole, piece[None], (x - k) % NX, 0)
    keep, give = take(whole, c, 2), take(whole, 1 - c, 2)
    got = swap_core(give)
    both = jnp.stack([jnp.where(c == 0, keep, got), jnp.where(c == 0, got, keep)], 1)
    rows = both.transpose(2, 3, 0, 1, 4).reshape(n, ROWS, NX * NC * HD)
    return [rows[i] for i in range(n)]


def up(value):
    return lax.ppermute(value, "z", [(i, i + 1) for i in range(NZ - 1)])


def down(value):
    return lax.ppermute(value, "z", [(i + 1, i) for i in range(NZ - 1)])


def across(value, flip):
    return lax.ppermute(value, "z", [(i, i ^ flip) for i in range(NZ)])


def sum_over(value, axis):
    return value + sum(lax.ppermute(value, axis, ring(axis, k)) for k in (1, 2, 3))


def smem():
    return pl.BlockSpec(memory_space=pltpu.SMEM)


def vmem():
    return pl.BlockSpec(memory_space=pltpu.VMEM)


def sds(shape, dtype):
    return jax.ShapeDtypeStruct(shape, dtype)


def per_device(queries, key_rows, value_rows, conv_key, conv_value, grad_out):
    z, x, c = lax.axis_index("z"), lax.axis_index("x"), lax.axis_index("c")
    head = x * NC + c
    zs = z.astype(jnp.int32).reshape(1)
    wk = lax.dynamic_slice_in_dim(conv_key, head * HD, HD, 2).reshape(4 * LEVELS, HD)
    wv = lax.dynamic_slice_in_dim(conv_value, head * HD, HD, 2).reshape(4 * LEVELS, HD)
    k0, v0 = rows_to_heads([key_rows[0], value_rows[0]])
    fine_l = up(jnp.stack([k0[-BLK:], v0[-BLK:]], 0))
    fine_r = down(jnp.stack([k0[:BLK], v0[:BLK]], 0))

    wide_shapes = [sds((PRE + HALO[l] + SIZES[l], HD), F32) for l in range(LEVELS)]
    own_shapes = [sds((SIZES[l], HD), BF16) for l in range(1, LEVELS + 1)]
    made = pl.pallas_call(
        coarse_kernel,
        out_shape=(wide_shapes + own_shapes) * 2,
        in_specs=[smem()] + [vmem()] * 6,
        out_specs=[vmem()] * (4 * LEVELS),
        compiler_params=PARAMS,
        name="coarsen",
    )(zs, k0, v0, fine_l[0, BLK - HALO[0] :], fine_l[1, BLK - HALO[0] :], wk, wv)
    wide_k, own_k = made[:LEVELS], made[LEVELS : 2 * LEVELS]
    wide_v, own_v = made[2 * LEVELS : 3 * LEVELS], made[3 * LEVELS :]

    coarse_l = up(jnp.stack([jnp.stack([own_k[i][-BLK:], own_v[i][-BLK:]], 0) for i in range(LEVELS - 1)], 0))
    coarse_r = down(jnp.stack([jnp.stack([own_k[i][:BLK], own_v[i][:BLK]], 0) for i in range(LEVELS - 1)], 0))
    last = jnp.stack([own_k[-1], own_v[-1]], 0)
    far = jnp.concatenate([across(last, 2), across(last, 3)], 1)
    q, do = rows_to_heads([queries[0], grad_out[0]])
    rim_l = jnp.concatenate([fine_l[None], coarse_l], 0)
    rim_r = jnp.concatenate([fine_r[None], coarse_r], 0)

    outs = pl.pallas_call(
        attention_kernel,
        out_shape=[
            sds((GROUP, HD), BF16),
            sds((GROUP, HD), BF16),
            sds((LEVELS, 2, BLK, HD), BF16),
            sds((LEVELS, 2, BLK, HD), BF16),
            sds((2, BLK, HD), BF16),
            sds((TOTAL, HD), F32),
            sds((TOTAL, HD), F32),
        ],
        in_specs=[smem()] + [vmem()] * (2 + 2 * LEVELS + 3),
        out_specs=[vmem()] * 7,
        scratch_shapes=[
            pltpu.VMEM((TOTAL, HD), BF16),
            pltpu.VMEM((TOTAL, HD), BF16),
            pltpu.VMEM((NBLK, HD, BLK), BF16),
            pltpu.VMEM((NBLK, HD, BLK), BF16),
            pltpu.VMEM((KEYS, 256), F32),
            pltpu.VMEM((KEYS, 256), BF16),
        ],
        compiler_params=PARAMS,
        name="attend",
    )(zs, q, do, k0, *own_k[:4], v0, *own_v[:4], rim_l, rim_r, far)
    att, dq, g_left, g_right, g_far, dk, dv = outs
    from_right = down(g_left)
    from_left = up(g_right)
    half = SIZES[LEVELS]
    far_a = across(g_far[:, :half], 2)
    far_b = across(g_far[:, half:], 3)
    attended, grad_query = heads_to_rows([att, dq])

    made = pl.pallas_call(
        back_kernel,
        out_shape=[
            sds((GROUP, HD), BF16),
            sds((GROUP, HD), BF16),
            sds((2, HALO[0], HD), BF16),
            sds((4 * LEVELS, HD), F32),
            sds((4 * LEVELS, HD), F32),
        ],
        in_specs=[vmem()] * (8 + 2 * LEVELS),
        out_specs=[vmem()] * 5,
        scratch_shapes=[pltpu.VMEM((HALO[l] + SIZES[l] + 8, HD), F32) for l in range(LEVELS + 1)],
        compiler_params=PARAMS,
        name="coarsen_back",
    )(dk, dv, from_left, from_right, far_a, far_b, wk, wv, *wide_k, *wide_v)
    gk, gv, halo, gwk, gwv = made
    halo = down(halo)
    gk = gk.at[-HALO[0] :].add(halo[0])
    gv = gv.at[-HALO[0] :].add(halo[1])
    grad_key, grad_value = heads_to_rows([gk, gv])

    gw = sum_over(sum_over(jnp.stack([gwk, gwv], 0), "z"), "y")
    whole = jnp.zeros((NX, 2, 4 * LEVELS, HD), F32)
    for k in range(NX):
        piece = lax.ppermute(gw, "x", ring("x", k)) if k else gw
        whole = lax.dynamic_update_slice_in_dim(whole, piece[None], (x - k) % NX, 0)
    other = swap_core(whole)
    both = jnp.stack([jnp.where(c == 0, whole, other), jnp.where(c == 0, other, whole)], 1)
    both = both.transpose(2, 3, 0, 1, 4).reshape(2, LEVELS, 4, NX * NC * HD)
    return attended[None], grad_query[None], grad_key[None], grad_value[None], both[0], both[1]


def solution(mesh):
    split = Mesh(mesh.devices.reshape(NZ, NX, NC, NY), ("z", "x", "c", "y"))
    rows = P("y", ("z", "x", "c"), None)
    return jax.shard_map(
        per_device,
        mesh=split,
        in_specs=(rows, rows, rows, P(), P(), rows),
        out_specs=(rows, rows, rows, rows, P(), P()),
        check_vma=False,
    )
```

```python
import math

import jax
import jax.numpy as jnp
from jax import lax
from jax.experimental import pallas as pl
from jax.experimental.pallas import tpu as pltpu
from jax.sharding import Mesh, PartitionSpec as P


HD = 128
BLK = 128
LEVELS = 5
NZ, NX, NC, NY = 4, 4, 2, 4
ROWS = 256
GROUP = ROWS * NX * NC
PAIRS = GROUP // 256
SIZES = [GROUP >> l for l in range(LEVELS + 1)]
HALO = [64 >> l for l in range(LEVELS + 1)]
PRE = 8
OFFS = [0]
for _l in range(LEVELS):
    OFFS.append(OFFS[-1] + SIZES[_l] + 2 * BLK)
TOTAL = OFFS[LEVELS] + BLK
NBLK = TOTAL // BLK
KEYS = 4 * BLK + 8 * BLK + BLK
SCALE = HD ** -0.5
EXPC = SCALE * math.log2(math.e)
NEG = -1e30
F32 = jnp.float32
BF16 = jnp.bfloat16
SLOTS = [(0, 0), (2, 0), (2, 1), (1, 0), (3, 0), (1, 1), (3, 1), (0, 1)]
MSG = LEVELS * 2 * BLK + 2 * SIZES[LEVELS]
PARAMS = pltpu.CompilerParams(vmem_limit_bytes=24 << 20)


def nn(a, b):
    return lax.dot_general(a, b, (((1,), (0,)), ((), ())), preferred_element_type=F32)


def nt(a, b):
    return lax.dot_general(a, b, (((1,), (1,)), ((), ())), preferred_element_type=F32)


def chunks(total, step):
    return [(r, min(step, total - r)) for r in range(0, total, step)]


def peer(pos_ref, slot):
    dx, dc = SLOTS[slot]
    return ((pos_ref[1] + dx) % NX) * NC + (pos_ref[2] + dc) % NC


def source(pos_ref, slot):
    dx, dc = SLOTS[slot]
    return ((pos_ref[1] + NX - dx) % NX) * NC + (pos_ref[2] + dc) % NC


def span(index, size):
    return pl.ds(pl.multiple_of(index * size, size), size)


def msg_rows(level, side):
    if level < LEVELS:
        start = (2 * level + side) * BLK
        return slice(start, start + BLK)
    start = 2 * LEVELS * BLK + side * SIZES[LEVELS]
    return slice(start, start + SIZES[LEVELS])


def pack_kernel(pos_ref, a_ref, b_ref, *outs):
    for slot, out in enumerate(outs):
        lanes = span(peer(pos_ref, slot), HD)
        out[0] = a_ref[0, :, lanes]
        out[1] = b_ref[0, :, lanes]


def unpack_kernel(pos_ref, *refs):
    slots, (a_ref, b_ref) = refs[:-2], refs[-2:]
    for slot, ref in enumerate(slots):
        lanes = span(source(pos_ref, slot), HD)
        a_ref[0, :, lanes] = ref[0]
        b_ref[0, :, lanes] = ref[1]


def back_pack_kernel(pos_ref, fine_ref, halo_ref, *outs):
    for slot, out in enumerate(outs):
        p = peer(pos_ref, slot)
        last = (p == NX * NC - 1).astype(F32)
        edge = ROWS - HALO[0]
        for side in range(2):
            out[side, 0:edge] = fine_ref[side, pl.ds(pl.multiple_of(p * ROWS, ROWS), edge), :]
            tail = fine_ref[side, pl.ds(pl.multiple_of(p * ROWS + edge, HALO[0]), HALO[0]), :]
            out[side, edge:ROWS] = (tail.astype(F32) + halo_ref[side].astype(F32) * last).astype(BF16)


def weights_kernel(pos_ref, *refs):
    slots, outs = refs[:-2], refs[-2:]
    for slot, ref in enumerate(slots):
        lanes = span(source(pos_ref, slot), HD)
        for side in range(2):
            for level in range(LEVELS):
                row = side * 4 * LEVELS + 4 * level
                outs[side][level, :, lanes] = ref[row : row + 4, :]


def coarse_kernel(pos_ref, halo_ref, wk_ref, wv_ref, *refs):
    pieces, outs = refs[: len(SLOTS)], refs[len(SLOTS) :]
    wides = (outs[0:LEVELS], outs[LEVELS : 2 * LEVELS])
    exts = outs[2 * LEVELS : 2 * LEVELS + 2]
    up_ref, down_ref, last_ref = outs[2 * LEVELS + 2 :]
    lanes = span(pos_ref[1] * NC + pos_ref[2], HD)
    for side in range(2):
        weight, wide, ext = (wk_ref, wv_ref)[side], wides[side], exts[side]
        x = wide[0]
        x[0:PRE, :] = jnp.zeros((PRE, HD), F32)
        x[PRE : PRE + HALO[0], :] = halo_ref[side].astype(F32)
        for slot, piece in enumerate(pieces):
            start = source(pos_ref, slot) * ROWS
            value = piece[side]
            x[pl.ds(pl.multiple_of(PRE + HALO[0] + start, 8), ROWS), :] = value.astype(F32)
            ext[pl.ds(pl.multiple_of(BLK + start, BLK), ROWS), :] = value
        for level in range(1, LEVELS + 1):
            x = wide[level - 1]
            taps = [weight[level - 1, j : j + 1, lanes] for j in range(4)]
            if level < LEVELS:
                wide[level][0:PRE, :] = jnp.zeros((PRE, HD), F32)
            first = 0 if level < LEVELS else HALO[level]
            for r, n in chunks(HALO[level] + SIZES[level] - first, 128):
                r += first
                acc = None
                for j in range(4):
                    term = taps[j] * x[pl.ds(PRE + 2 * r - 2 + j, n, stride=2), :]
                    acc = term if acc is None else acc + term
                low = acc.astype(BF16)
                if level < LEVELS:
                    wide[level][PRE + r : PRE + r + n, :] = low.astype(F32)
                else:
                    for ref in (up_ref, down_ref):
                        ref[msg_rows(LEVELS, side), :] = low
                    last_ref[side * n : (side + 1) * n, :] = low
            if level < LEVELS:
                for r, n in chunks(SIZES[level], 256):
                    start = PRE + HALO[level] + r
                    to = OFFS[level] + BLK + r
                    ext[to : to + n, :] = wide[level][start : start + n, :].astype(BF16)
        for level in range(LEVELS):
            begin = OFFS[level] + BLK
            end = begin + SIZES[level]
            down_ref[msg_rows(level, side), :] = ext[begin : begin + BLK, :]
            up_ref[msg_rows(level, side), :] = ext[end - BLK : end, :]


def attention_kernel(pos_ref, *refs):
    n = len(SLOTS)
    pieces = refs[:n]
    k_in, v_in, from_below, from_above, far_ref = refs[n : n + 5]
    sends = refs[n + 5 : 2 * n + 5]
    up_ref, down_ref, gfar_ref, dk_ref, dv_ref = refs[2 * n + 5 : 2 * n + 10]
    kx, vx, kt, vt, s_ref, e_ref, q_ref, do_ref, att_ref, dq_ref = refs[2 * n + 10 :]
    z = pos_ref[0]
    half = SIZES[LEVELS]
    far = OFFS[LEVELS]
    even = z % 2 == 0
    for slot, piece in enumerate(pieces):
        rows = span(source(pos_ref, slot), ROWS)
        q_ref[rows, :] = piece[0]
        do_ref[rows, :] = piece[1]
    for side, (own, ext, tr, grad) in enumerate(((k_in, kx, kt, dk_ref), (v_in, vx, vt, dv_ref))):
        for level in range(LEVELS):
            begin = OFFS[level] + BLK
            end = begin + SIZES[level]
            ext[begin - BLK : begin, :] = from_below[msg_rows(level, side), :]
            for r, m in chunks(SIZES[level], 256):
                ext[begin + r : begin + r + m, :] = own[begin + r : begin + r + m, :]
            ext[end : end + BLK, :] = from_above[msg_rows(level, side), :]
        ext[far : far + half, :] = far_ref[side * half : (side + 1) * half, :]
        rows = msg_rows(LEVELS, side)
        ext[far + half : far + 2 * half, :] = jnp.where(even, from_below[rows, :], from_above[rows, :])

        def prepare(i, _, ext=ext, tr=tr, grad=grad):
            rows = span(i, BLK)
            tr[i] = ext[rows, :].T
            grad[rows, :] = jnp.zeros((BLK, HD), F32)
            return 0

        lax.fori_loop(0, NBLK, prepare, 0)

    lane = lax.broadcasted_iota(jnp.int32, (BLK, 2 * BLK), 1)

    def pair(p, _):
        qrows = pl.ds(pl.multiple_of(p * 256, 256), 256)
        qt = q_ref[qrows, :].T
        dot_t = do_ref[qrows, :].astype(F32).T
        groups = [[2 * p + i for i in range(4)]]
        valid = [None]
        for level in range(1, LEVELS):
            c = p >> (level - 1)
            base = OFFS[level] // BLK
            groups.append([base + c, base + c + 2])
            count = SIZES[level] // BLK
            valid.append((jnp.logical_or(c > 0, z > 0), jnp.logical_or(c < count - 1, z < NZ - 1)))
        groups.append([OFFS[LEVELS] // BLK])
        valid.append((None,))

        def rows_of(ext, blocks, contiguous):
            if contiguous:
                return ext[pl.ds(pl.multiple_of(blocks[0] * BLK, BLK), BLK * len(blocks)), :]
            parts = [ext[pl.ds(pl.multiple_of(b * BLK, BLK), BLK), :] for b in blocks]
            return parts[0] if len(parts) == 1 else jnp.concatenate(parts, 0)

        def cols_of(tr, blocks):
            parts = [tr[b] for b in blocks]
            return parts[0] if len(parts) == 1 else jnp.concatenate(parts, 1)

        top = jnp.full((8, 256), NEG, F32)
        row = 0
        for gid, blocks in enumerate(groups):
            n = BLK * len(blocks)
            s = nn(rows_of(kx, blocks, gid == 0), qt)
            for i in range(len(blocks)):
                part = s[i * BLK : (i + 1) * BLK, :]
                if gid == 0 and i == 0:
                    lim = jnp.where(jnp.logical_or(p > 0, z > 0), BLK, 0)
                    part = jnp.where(lane < lim, part, NEG)
                elif gid == 0 and i == 3:
                    lim = jnp.where(jnp.logical_or(p < PAIRS - 1, z < NZ - 1), BLK, 2 * BLK)
                    part = jnp.where(lane >= lim, part, NEG)
                elif gid > 0 and valid[gid][i] is not None:
                    part = jnp.where(valid[gid][i], part, NEG)
                s_ref[row + i * BLK : row + (i + 1) * BLK, :] = part
                top = jnp.maximum(top, jnp.max(part.reshape(BLK // 8, 8, 256), 0))
            row += n
        shift = jnp.max(top, 0, keepdims=True) * EXPC
        total = jnp.zeros((8, 256), F32)
        out_t = jnp.zeros((HD, 256), F32)
        row = 0
        for blocks in groups:
            n = BLK * len(blocks)
            e = jnp.exp2(s_ref[row : row + n, :] * EXPC - shift)
            total = total + jnp.sum(e.reshape(n // 8, 8, 256), 0)
            low = e.astype(BF16)
            e_ref[row : row + n, :] = low
            out_t = out_t + nn(cols_of(vt, blocks), low)
            row += n
        inverse = 1.0 / jnp.sum(total, 0, keepdims=True)
        out_t = out_t * inverse
        att_ref[qrows, :] = out_t.T.astype(BF16)
        don_t = (dot_t * inverse).astype(BF16)
        delta = jnp.sum(don_t.astype(F32) * out_t, 0, keepdims=True)
        dq_t = jnp.zeros((HD, 256), F32)
        row = 0
        for gid, blocks in enumerate(groups):
            n = BLK * len(blocks)
            low = e_ref[row : row + n, :]
            dp = nn(rows_of(vx, blocks, gid == 0), don_t)
            ds = (low.astype(F32) * (dp - delta)).astype(BF16)
            dq_t = dq_t + nn(cols_of(kt, blocks), ds)
            dk = nt(ds, qt)
            dv = nt(low, don_t)
            for i, b in enumerate(blocks):
                rows = pl.ds(pl.multiple_of(b * BLK, BLK), BLK)
                dk_ref[rows, :] += dk[i * BLK : (i + 1) * BLK, :]
                dv_ref[rows, :] += dv[i * BLK : (i + 1) * BLK, :]
            row += n
        dq_ref[qrows, :] = (dq_t * SCALE).T.astype(BF16)
        return 0

    lax.fori_loop(0, PAIRS, pair, 0)
    for side, (grad, mult) in enumerate(((dk_ref, SCALE), (dv_ref, 1.0))):
        for level in range(LEVELS):
            begin = OFFS[level] + BLK
            end = begin + SIZES[level]
            down_ref[msg_rows(level, side), :] = (grad[begin - BLK : begin, :] * mult).astype(BF16)
            up_ref[msg_rows(level, side), :] = (grad[end : end + BLK, :] * mult).astype(BF16)
        gfar_ref[side * half : (side + 1) * half, :] = (grad[far : far + half, :] * mult).astype(BF16)
        other = (grad[far + half : far + 2 * half, :] * mult).astype(BF16)
        for ref in (up_ref, down_ref):
            ref[msg_rows(LEVELS, side), :] = other
    for slot, send in enumerate(sends):
        rows = span(peer(pos_ref, slot), ROWS)
        send[0] = att_ref[rows, :]
        send[1] = dq_ref[rows, :]


def back_kernel(pos_ref, dk_ref, dv_ref, from_left, from_right, far_ref, wk_ref, wv_ref, *refs):
    xs = (refs[0:LEVELS], refs[LEVELS : 2 * LEVELS])
    fine_out, halo_out, gw_out = refs[2 * LEVELS : 2 * LEVELS + 3]
    g = refs[2 * LEVELS + 3 :]
    half = SIZES[LEVELS]
    even = pos_ref[0] % 2 == 0
    lanes = span(pos_ref[1] * NC + pos_ref[2], HD)
    for side in range(2):
        weight = (wk_ref, wv_ref)[side]
        grad = (dk_ref, dv_ref)[side]
        mult = (SCALE, 1.0)[side]
        base = side * 4 * LEVELS
        end = HALO[LEVELS] + SIZES[LEVELS]
        g[LEVELS][0 : HALO[LEVELS], :] = jnp.zeros((HALO[LEVELS], HD), F32)
        g[LEVELS][HALO[LEVELS] : end, :] = (
            far_ref[side * half : (side + 1) * half, :].astype(F32)
            + jnp.where(even, from_left[msg_rows(LEVELS, side), :], from_right[msg_rows(LEVELS, side), :]).astype(F32)
        )
        g[LEVELS][end : end + 8, :] = jnp.zeros((8, HD), F32)
        for level in range(LEVELS, 0, -1):
            taps = [weight[level - 1, j : j + 1, lanes] for j in range(4)]
            x = xs[side][level - 1]
            here, below = g[level], g[level - 1]
            sums = [jnp.zeros((8, HD), F32) for _ in range(4)]
            total = HALO[level] + SIZES[level]
            for r, n in chunks(total, 128):
                g0 = here[r : r + n, :]
                g1 = here[r + 1 : r + n + 1, :]
                below[pl.ds(2 * r, n, stride=2), :] = taps[2] * g0 + taps[0] * g1
                below[pl.ds(2 * r + 1, n, stride=2), :] = taps[3] * g0 + taps[1] * g1
                for j in range(4):
                    prod = g0 * x[pl.ds(PRE + 2 * r - 2 + j, n, stride=2), :]
                    if n % 8 == 0:
                        sums[j] = sums[j] + jnp.sum(prod.reshape(n // 8, 8, HD), 0)
                    else:
                        gap = jnp.zeros((8 - n % 8, HD), F32)
                        prod = jnp.concatenate([prod, gap], 0)
                        sums[j] = sums[j] + jnp.sum(prod.reshape((n + 7) // 8, 8, HD), 0)
            for j in range(4):
                row = base + 4 * (level - 1) + j
                gw_out[row : row + 1, :] = jnp.sum(sums[j], 0, keepdims=True)
            low = level - 1
            off = OFFS[low] + BLK
            size, pad = SIZES[low], HALO[low]
            for r, n in chunks(size, 128):
                value = below[pad + r : pad + r + n, :] + grad[off + r : off + r + n, :] * mult
                if r == 0:
                    value = value + from_left[msg_rows(low, side), :].astype(F32)
                if r == size - BLK:
                    value = value + from_right[msg_rows(low, side), :].astype(F32)
                if low > 0:
                    below[pad + r : pad + r + n, :] = value
                else:
                    fine_out[side, r : r + n, :] = value.astype(BF16)
            if low > 0:
                below[pad + size : pad + size + 8, :] = jnp.zeros((8, HD), F32)
            else:
                halo_out[side] = below[0:pad, :].astype(BF16)


def exchange(slots):
    received = [slots[0]]
    for i, (dx, dc) in enumerate(SLOTS[1:], 1):
        pairs = [(x * NC + c, (x + dx) % NX * NC + (c + dc) % NC) for x in range(NX) for c in range(NC)]
        received.append(lax.ppermute(slots[i], ("x", "c"), pairs))
    return received


def ring(value, axis, k, size=4):
    return lax.ppermute(value, axis, [(i, (i + k) % size) for i in range(size)])


def across(value, flip):
    return lax.ppermute(value, "z", [(i, i ^ flip) for i in range(NZ)])


def sum_over(value, axis):
    return value + sum(ring(value, axis, k) for k in (1, 2, 3))


def smem():
    return pl.BlockSpec(memory_space=pltpu.SMEM)


def vmem():
    return pl.BlockSpec(memory_space=pltpu.VMEM)


def sds(shape, dtype):
    return jax.ShapeDtypeStruct(shape, dtype)


def call(kernel, out_shape, pos, *args, scratch=()):
    return pl.pallas_call(
        kernel,
        out_shape=out_shape,
        in_specs=[smem()] + [vmem()] * len(args),
        out_specs=[vmem()] * len(out_shape),
        scratch_shapes=list(scratch),
        compiler_params=PARAMS,
    )(pos, *args)


def layer(queries, key_rows, value_rows, conv_key, conv_value, grad_out):
    z, x, c = lax.axis_index("z"), lax.axis_index("x"), lax.axis_index("c")
    pos = jnp.stack([z, x, c]).astype(jnp.int32)
    slot_shape = [sds((2, ROWS, HD), BF16)] * len(SLOTS)
    row_shape = [sds((1, ROWS, NX * NC * HD), BF16)] * 2
    msg = sds((MSG, HD), BF16)
    far_shape = sds((2 * SIZES[LEVELS], HD), BF16)
    ext_shape = sds((TOTAL, HD), BF16)
    ext_grad = sds((TOTAL, HD), F32)

    kv = exchange(call(pack_kernel, slot_shape, pos, key_rows, value_rows))
    halo = jnp.zeros((2, HALO[0], HD), BF16)
    for (dx, dc), piece in zip(SLOTS, kv):
        here = jnp.logical_and((x + 1) % NX == dx, (c + dc) % NC == 1)
        halo = jnp.where(here, piece[:, ROWS - HALO[0] :], halo)
    qd = call(pack_kernel, slot_shape, pos, queries, grad_out)
    halo, *qd = lax.optimization_barrier((halo, *qd))
    halo = lax.ppermute(halo, "z", [(i, i + 1) for i in range(NZ - 1)])
    qd = exchange(qd)

    wides = [sds((PRE + HALO[l] + SIZES[l], HD), F32) for l in range(LEVELS)] * 2
    made = call(
        coarse_kernel, wides + [ext_shape, ext_shape, msg, msg, far_shape], pos, halo, conv_key, conv_value, *kv
    )
    wides, (k_ext, v_ext, up, down, last) = made[: 2 * LEVELS], made[2 * LEVELS :]
    from_below, from_above = ring(up, "z", 1), ring(down, "z", 3)
    far = across(last, 2)

    scratch = [
        pltpu.VMEM((TOTAL, HD), BF16),
        pltpu.VMEM((TOTAL, HD), BF16),
        pltpu.VMEM((NBLK, HD, BLK), BF16),
        pltpu.VMEM((NBLK, HD, BLK), BF16),
        pltpu.VMEM((KEYS, 256), F32),
        pltpu.VMEM((KEYS, 256), BF16),
    ] + [pltpu.VMEM((GROUP, HD), BF16)] * 4
    made = call(
        attention_kernel, slot_shape + [msg, msg, far_shape, ext_grad, ext_grad],
        pos, *qd, k_ext, v_ext, from_below, from_above, far, scratch=scratch,
    )
    sends, (up, down, far, dk, dv) = made[: len(SLOTS)], made[len(SLOTS) :]
    from_left, from_right = ring(up, "z", 1), ring(down, "z", 3)
    far = across(far, 2)
    attended, grad_query = call(unpack_kernel, row_shape, pos, *exchange(sends))

    fine, halo, gw = call(
        back_kernel,
        [sds((2, GROUP, HD), BF16), sds((2, HALO[0], HD), BF16), sds((8 * LEVELS, HD), F32)],
        pos, dk, dv, from_left, from_right, far, conv_key, conv_value, *wides,
        scratch=[pltpu.VMEM((HALO[l] + SIZES[l] + 8, HD), F32) for l in range(LEVELS + 1)],
    )
    halo = lax.ppermute(halo, "z", [(i + 1, i) for i in range(NZ - 1)])
    sends = call(back_pack_kernel, slot_shape, pos, fine, halo)
    grad_key, grad_value = call(unpack_kernel, row_shape, pos, *exchange(sends))

    gw = sum_over(sum_over(gw, "z"), "y")
    weight_shape = [sds((LEVELS, 4, NX * NC * HD), F32)] * 2
    grad_ck, grad_cv = call(weights_kernel, weight_shape, pos, *exchange([gw] * len(SLOTS)))
    return attended, grad_query, grad_key, grad_value, grad_ck, grad_cv


def solution(mesh):
    split = Mesh(mesh.devices.reshape(NZ, NX, NC, NY), ("z", "x", "c", "y"))
    rows = P("y", ("z", "x", "c"), None)
    return jax.shard_map(
        layer,
        mesh=split,
        in_specs=(rows, rows, rows, P(), P(), rows),
        out_specs=(rows, rows, rows, rows, P(), P()),
        check_vma=False,
    )
```
